256 devices in a mesh: dp: 2 (over core), expert: 128 (over z, x, y).
Axes of the slice: x: 4, y: 4, z: 8, core: 2. Of those that a mesh axis runs over, the one named last changes fastest.
Arguments:
- tokens: bfloat16 [32768, 2048], P(('dp', 'expert')), may hold values from -6 to 6
- out_grad: bfloat16 [32768, 2048], P(('dp', 'expert')), may hold values from -6 to 6
- expert_ids: int32 [32768, 4], P(('dp', 'expert')), may hold values from 0 to 127, as said below
- gate_weights: float32 [32768, 4], P(('dp', 'expert')), may hold values from 0.05 to 0.6
- w_in: bfloat16 [128, 2048, 768], P('expert'), may hold values from -0.125 to 0.125
- w_out: bfloat16 [128, 384, 2048], P('expert'), may hold values from -0.3125 to 0.3125
Outputs:
- token_grad: bfloat16 [32768, 2048], P(('dp', 'expert'))
- w_in_grad: bfloat16 [128, 2048, 768], P('expert', 'dp')
- w_out_grad: bfloat16 [128, 384, 2048], P('expert', None, 'dp')
The draws below stay inside these ranges and needn't reach their ends.
Inputs may be any that keep to these rules, and one draw needn't show every extreme that they name: `expert_ids`: each token names 4 different experts; among the 128 tokens of one device no expert is named more than 7 times, and in every device's tokens some expert is named exactly 7 times.
All inputs are finite; a program needn't handle non-finite values.
Results may differ from the reference program's by a relative error of at most 0.0065.
Values may be sent and summed in bfloat16 or wider, within the bound.
No kernel may reach another device: no remote copies, remote signals or barrier semaphores. Data moves between devices by JAX's collectives and lax.ppermute only.
A program may use at most 128 MiB of HBM per device.

```python
import math
import jax
import jax.numpy as jnp
from jax import lax

D = 2048
FF = 384
ROUTES = 4
TOK_DEV = 128
EXPERTS = 128
CAP = 7
TOKENS = 32768
DEVICES = 256


def draw_expert_ids(key, part):
    block_count = TOKENS // TOK_DEV
    order = jax.random.permutation(jax.random.fold_in(key, 11), EXPERTS).astype(jnp.int32)
    offset = jax.random.randint(jax.random.fold_in(key, 12), (block_count,), 0, EXPERTS - 1).astype(jnp.int32)
    block_index = jnp.arange(block_count, dtype=jnp.int32)
    chosen = order[block_index % EXPERTS]
    slot = jnp.arange(TOK_DEV * ROUTES, dtype=jnp.int32)
    marked_before = jnp.minimum((slot + ROUTES - 1) // ROUTES, CAP)
    marked = (slot % ROUTES == 0) & (slot // ROUTES < CAP)
    others = slot - marked_before
    rest = (chosen[:, None] + 1 + (offset[:, None] + others[None, :]) % (EXPERTS - 1)) % EXPERTS
    picked = jnp.where(marked[None, :], chosen[:, None], rest)
    return picked.reshape(TOKENS, ROUTES).astype(jnp.int32)


def levels(own_key, dims, split, smallest, high):
    factor_of, own = 1.0, jax.random.fold_in(own_key, 6)
    for position, shards_of in split:
        draws = jnp.exp(jax.random.uniform(jax.random.fold_in(own, position), (shards_of,), jnp.float32, smallest / len(split), high / len(split)))
        factor_of = factor_of * jnp.repeat(draws, dims[position] // shards_of).reshape([-1 if axis == position else 1 for axis in range(len(dims))])
    return factor_of


def noise(own_key, extent, deviation, reach, split=(), kind=jnp.bfloat16):
    result = deviation * jax.random.normal(own_key, extent, jnp.float32)
    if split:
        result = result * levels(own_key, extent, split, -0.22, 0.18)
    return jnp.clip(result, -reach, reach).astype(kind)


def setup_inputs(seed: int = 0) -> dict:
    splits = jax.random.split(jax.random.key(seed), 7)
    tokens = noise(splits[0], (TOKENS, D), 1.0, 6.0, ((0, 256),))
    out_grad = noise(splits[1], (TOKENS, D), 1.0, 6.0, ((0, 256),))
    expert_ids = draw_expert_ids(jax.random.fold_in(splits[6], 71), 0)
    gate_weights = jnp.clip(jnp.exp(math.log(0.6) - 2.4849067 * jax.random.uniform(splits[3], (TOKENS, ROUTES), jnp.float32) ** levels(splits[3], (TOKENS, ROUTES), ((0, 256),), -0.2, 0.2)), 0.05, 0.6)
    w_in = noise(splits[4], (EXPERTS, D, 2 * FF), D ** -0.5, 0.125, ((0, 128),))
    w_out = noise(splits[5], (EXPERTS, FF, D), FF ** -0.5, 0.3125, ((0, 128),))
    return {"tokens": tokens, "out_grad": out_grad, "expert_ids": expert_ids, "gate_weights": gate_weights, "w_in": w_in, "w_out": w_out}


def silu_parts(gate_part):
    sigma = 1.0 / (1.0 + jnp.exp(-gate_part))
    return gate_part * sigma, sigma * (1.0 + gate_part * (1.0 - sigma))


def expert_back(rows_in, rows_grad, weight_in, weight_out):
    hidden_width = weight_out.shape[0]
    joined = jnp.dot(rows_in, weight_in, preferred_element_type=jnp.float32)
    gate_part = joined[:, :hidden_width]
    up_part = joined[:, hidden_width:]
    activated, derivative = silu_parts(gate_part)
    hidden = (activated * up_part).astype(jnp.bfloat16)
    d_hidden = lax.dot_general(rows_grad, weight_out, (((1,), (1,)), ((), ())), preferred_element_type=jnp.float32)
    d_joined = jnp.concatenate([d_hidden * up_part * derivative, d_hidden * activated], axis=1).astype(jnp.bfloat16)
    d_rows = lax.dot_general(d_joined, weight_in, (((1,), (1,)), ((), ())), preferred_element_type=jnp.float32).astype(jnp.bfloat16)
    grad_in = lax.dot_general(rows_in, d_joined, (((0,), (0,)), ((), ())), preferred_element_type=jnp.float32)
    grad_out = lax.dot_general(hidden, rows_grad, (((0,), (0,)), ((), ())), preferred_element_type=jnp.float32)
    return d_rows, grad_in, grad_out


def reference(tokens, out_grad, expert_ids, gate_weights, w_in, w_out):
    flat_ids = expert_ids.reshape(-1).astype(jnp.int32)
    total_routes = flat_ids.shape[0]
    route_tok = (jnp.arange(total_routes, dtype=jnp.int32) // ROUTES).astype(jnp.int32)
    gate_flat = gate_weights.reshape(-1)
    sorted_routes = jnp.argsort(flat_ids, stable=True).astype(jnp.int32)
    counts = jnp.bincount(flat_ids, length=EXPERTS).astype(jnp.int32)
    offsets = (jnp.cumsum(counts) - counts).astype(jnp.int32)
    most_rows = DEVICES * CAP
    padded = jnp.concatenate([sorted_routes, jnp.zeros((most_rows,), jnp.int32)])

    def per_expert(carry, expert):
        route_index = lax.dynamic_slice(padded, (offsets[expert].astype(jnp.int32),), (most_rows,))
        live_rows = jnp.arange(most_rows, dtype=jnp.int32) < counts[expert]
        token_rows = route_tok[route_index]
        rows_in = tokens[token_rows]
        scaled = gate_flat[route_index][:, None] * out_grad[token_rows].astype(jnp.float32)
        rows_grad = jnp.where(live_rows[:, None], scaled, jnp.zeros((), jnp.float32)).astype(jnp.bfloat16)
        d_rows, grad_in, grad_out = expert_back(rows_in, rows_grad, w_in[expert], w_out[expert])
        carry = carry.at[token_rows].add(d_rows.astype(jnp.float32))
        return carry, (grad_in.astype(jnp.bfloat16), grad_out.astype(jnp.bfloat16))

    start = jnp.zeros(tokens.shape, jnp.float32)
    summed, grads = lax.scan(per_expert, start, jnp.arange(EXPERTS, dtype=jnp.int32))
    return summed.astype(jnp.bfloat16), grads[0], grads[1]
```

```python
import jax
import jax.numpy as jnp
from jax import lax
from jax.sharding import Mesh
from jax.sharding import PartitionSpec as P

Z, X, Y = 8, 4, 4
PLANE = X * Y
CAP = 7
IN_CHUNKS = 1
GRAD_CHUNKS = 1
BACK_CHUNKS = 1

f32 = jnp.float32
bf16 = jnp.bfloat16


def mm(a, b, ca, cb):
    return lax.dot_general(a, b, (((ca,), (cb,)), ((), ())), preferred_element_type=f32)


def pieces(width, count):
    step = width // count
    return [(i * step, (i + 1) * step) for i in range(count)]


def silu_parts(gate_part):
    sigma = 1.0 / (1.0 + jnp.exp(-gate_part))
    return gate_part * sigma, sigma * (1.0 + gate_part * (1.0 - sigma))


def routing(meta, plane):
    sources, tok = Z, meta.shape[-1]
    meta = meta.reshape(sources, 8, tok)
    ids = meta[:, :4].astype(jnp.int32)
    gates = meta[:, 4:]
    local = plane * PLANE + jnp.arange(PLANE, dtype=jnp.int32)
    match = ids[:, :, None, :] == local[None, None, :, None]
    named = jnp.any(match, axis=1)
    gate = jnp.sum(jnp.where(match, gates[:, :, None, :], 0.0), axis=1)
    index = jnp.arange(tok, dtype=jnp.int32)
    earlier = (index[:, None] < index[None, :]).astype(bf16)
    before = mm(named.astype(bf16).reshape(sources * PLANE, tok), earlier, 1, 0)
    rank = jnp.where(named, before.reshape(sources, PLANE, tok), -1.0)
    rank = rank.transpose(1, 0, 2)
    gate = gate.transpose(1, 0, 2)
    slot_rank = jnp.arange(CAP, dtype=jnp.int32).astype(f32)
    hit = rank[:, None] == slot_rank[None, :, None, None]
    slot_gate = jnp.sum(jnp.where(hit, gate[:, None], 0.0), axis=3).reshape(-1, 1)
    same = jnp.arange(sources)[:, None] == jnp.arange(sources)[None, :]
    wide = jnp.where(same[None, :, :, None], rank[:, None], -1.0).reshape(PLANE, 1, sources, sources * tok)
    slots = (wide == slot_rank[None, :, None, None]).astype(bf16)
    return slots.reshape(PLANE * CAP * sources, sources * tok), slot_gate


def body(tokens, out_grad, expert_ids, gate_weights, w_in, w_out):
    width = tokens.shape[1]
    w_in, w_out = w_in[0], w_out[0]
    half = w_out.shape[0]
    plane = lax.axis_index("z")
    core = lax.axis_index("dp")

    def gather_z(x):
        return lax.all_gather(x, "z", axis=0, tiled=True)

    def swap_plane(x):
        return lax.all_to_all(x, ("x", "y"), split_axis=0, concat_axis=0, tiled=True)

    meta = gather_z(jnp.concatenate([expert_ids.astype(f32), gate_weights], axis=1).T)
    slots, slot_gate = routing(meta, plane)

    rows_in = []
    for lo, hi in pieces(width, IN_CHUNKS):
        every = gather_z(tokens[:, lo:hi])
        rows_in.append(swap_plane(mm(slots, every, 1, 0).astype(bf16)))
    rows_grad = []
    for lo, hi in pieces(width, GRAD_CHUNKS):
        every = gather_z(out_grad[:, lo:hi])
        rows_grad.append(swap_plane((mm(slots, every, 1, 0) * slot_gate).astype(bf16)))

    joined = sum(mm(r, w_in[lo:hi], 1, 0) for r, (lo, hi) in zip(rows_in, pieces(width, IN_CHUNKS)))
    d_hidden = sum(mm(r, w_out[:, lo:hi], 1, 1) for r, (lo, hi) in zip(rows_grad, pieces(width, GRAD_CHUNKS)))
    gate_part, up_part = joined[:, :half], joined[:, half:]
    activated, derivative = silu_parts(gate_part)
    hidden = (activated * up_part).astype(bf16)
    d_joined = jnp.concatenate([d_hidden * up_part * derivative, d_hidden * activated], axis=1).astype(bf16)

    token_grad = []
    for lo, hi in pieces(width, BACK_CHUNKS):
        back = swap_plane(mm(d_joined, w_in[lo:hi], 1, 1).astype(bf16))
        part = mm(slots, back, 0, 0).astype(bf16)
        token_grad.append(lax.psum_scatter(part, "z", scatter_dimension=0, tiled=True))
    token_grad = jnp.concatenate(token_grad, axis=1)

    grad_in = mm(jnp.concatenate(rows_in, axis=1), d_joined, 0, 0)
    grad_out = mm(hidden, jnp.concatenate(rows_grad, axis=1), 0, 0)
    half_width = width // 2
    other = 1 - core

    def sum_cores(x, axis):
        keep = lax.dynamic_slice_in_dim(x, core * half_width, half_width, axis)
        send = lax.dynamic_slice_in_dim(x, other * half_width, half_width, axis)
        got = lax.ppermute(send, "dp", [(0, 1), (1, 0)])
        return (keep + got).astype(bf16)[None]

    return token_grad, sum_cores(grad_in, 0), sum_cores(grad_out, 1)


def solution(mesh):
    split = Mesh(mesh.devices.reshape(2, Z, X, Y), ("dp", "z", "x", "y"))
    hosts = ("z", "x", "y")
    rows = P(("dp",) + hosts, None)
    in_specs = (rows, rows, rows, rows, P(hosts, None, None), P(hosts, None, None))
    out_specs = (rows, P(hosts, "dp", None), P(hosts, None, "dp"))
    return jax.shard_map(body, mesh=split, in_specs=in_specs, out_specs=out_specs, check_vma=False)
```

```python
import jax
import jax.numpy as jnp
from jax import lax
from jax.experimental import pallas as pl
from jax.experimental.pallas import tpu as pltpu
from jax.sharding import Mesh
from jax.sharding import PartitionSpec as P

Z, X, Y = 8, 4, 4
PLANE = X * Y
CAP = 7
SLOTS = PLANE * CAP * Z
GRAD_FIRST = 512

f32 = jnp.float32
bf16 = jnp.bfloat16


def mm(a, b, ca, cb):
    return lax.dot_general(a, b, (((ca,), (cb,)), ((), ())), preferred_element_type=f32)


def silu_parts(gate_part):
    sigma = 1.0 / (1.0 + jnp.exp(-gate_part))
    return gate_part * sigma, sigma * (1.0 + gate_part * (1.0 - sigma))


def rank_table(ids, gates, local):
    sources, _, tok = ids.shape
    match = ids[:, :, None, :] == local[None, None, :, None]
    named = jnp.any(match, axis=1)
    gate = jnp.sum(jnp.where(match, gates[:, :, None, :], 0.0), axis=1)
    index = jnp.arange(tok, dtype=jnp.int32)
    earlier = (index[:, None] < index[None, :]).astype(bf16)
    before = mm(named.astype(bf16).reshape(-1, tok), earlier, 1, 0)
    return jnp.where(named, before.reshape(named.shape), -1.0), gate


def plane_slots(meta, plane):
    tok = meta.shape[-1]
    meta = meta.reshape(Z, 8, tok)
    local = plane * PLANE + jnp.arange(PLANE, dtype=jnp.int32)
    rank, gate = rank_table(meta[:, :4].astype(jnp.int32), meta[:, 4:], local)
    rank, gate = rank.transpose(1, 0, 2), gate.transpose(1, 0, 2)
    slot_rank = jnp.arange(CAP, dtype=jnp.int32).astype(f32)
    hit = rank[:, None] == slot_rank[None, :, None, None]
    slot_gate = jnp.sum(jnp.where(hit, gate[:, None], 0.0), axis=3).reshape(-1, 1)
    same = jnp.arange(Z)[:, None] == jnp.arange(Z)[None, :]
    wide = jnp.where(same[None, :, :, None], rank[:, None], -1.0).reshape(PLANE, 1, Z, Z * tok)
    slots = (wide == slot_rank[None, :, None, None]).astype(bf16)
    return slots.reshape(SLOTS, Z * tok), slot_gate


def column_slots(ids, gates):
    tok = ids.shape[-1]
    rank, gate = rank_table(ids[None], gates[None], jnp.arange(Z * PLANE, dtype=jnp.int32))
    rank = rank.reshape(Z, PLANE, tok).transpose(1, 0, 2)
    gate = gate.reshape(Z, PLANE, tok).transpose(1, 0, 2)
    slot_rank = jnp.arange(CAP, dtype=jnp.int32).astype(f32)
    hit = rank[:, None] == slot_rank[None, :, None, None]
    slot_gate = jnp.sum(jnp.where(hit, gate[:, None], 0.0), axis=3).reshape(-1, 1)
    return hit.astype(bf16).reshape(SLOTS, tok), slot_gate


def order_matrices(plane):
    rows = PLANE * CAP
    by_distance = lax.broadcasted_iota(jnp.int32, (SLOTS, SLOTS), 0)
    by_plane = lax.broadcasted_iota(jnp.int32, (SLOTS, SLOTS), 1)
    same_row = by_plane // Z == by_distance % rows
    at = by_plane % Z
    distance = by_distance // rows
    to_send = same_row & (at == (plane + distance) % Z)
    by_plane, by_distance = by_distance, by_plane
    received = (by_plane // Z == by_distance % rows) & (by_plane % Z == (plane + Z - by_distance // rows) % Z)
    return to_send.astype(bf16), received.astype(bf16)


def times(name, matrix, parts, tile):
    width = parts[0].shape[1]

    def kernel(matrix_ref, *refs):
        stacked = jnp.concatenate([ref[...] for ref in refs[:-1]], axis=0)
        refs[-1][...] = jnp.dot(matrix_ref[...], stacked, preferred_element_type=f32).astype(bf16)

    return pl.pallas_call(
        kernel,
        grid=(width // tile,),
        in_specs=[pl.BlockSpec(matrix.shape, lambda i: (0, 0))] + [pl.BlockSpec((p.shape[0], tile), lambda i: (0, i)) for p in parts],
        out_specs=pl.BlockSpec((matrix.shape[0], tile), lambda i: (0, i)),
        out_shape=jax.ShapeDtypeStruct((matrix.shape[0], width), bf16),
        compiler_params=pltpu.CompilerParams(vmem_limit_bytes=24 * 2**20),
        name=name,
    )(matrix, *parts)


def weave(received, parts):
    return times("weave", received, parts, 512)


def body(tokens, out_grad, expert_ids, gate_weights, w_in, w_out):
    width = tokens.shape[1]
    w_in, w_out = w_in[0], w_out[0]
    half = w_out.shape[0]
    plane = lax.axis_index("z")
    core = lax.axis_index("dp")

    def gather_z(x):
        return lax.all_gather(x, "z", axis=0, tiled=True)

    def swap_plane(x):
        return lax.all_to_all(x, ("x", "y"), split_axis=0, concat_axis=0, tiled=True)

    def swap_z(x):
        rows = PLANE * CAP
        parts = [x[:rows]]
        for distance in range(1, Z):
            piece = x[distance * rows : (distance + 1) * rows]
            parts.append(lax.ppermute(piece, "z", [(i, (i + distance) % Z) for i in range(Z)]))
        return parts

    ids = expert_ids.T
    gates = gate_weights.T
    own_slots, own_gate = lax.optimization_barrier(column_slots(ids, gates))
    to_send, received = lax.optimization_barrier(order_matrices(plane))

    tokens_all = gather_z(tokens)
    first = (mm(own_slots, out_grad[:, :GRAD_FIRST], 1, 0) * own_gate).astype(bf16)
    meta = jnp.concatenate([ids.astype(f32), gates], axis=0)
    meta, rest = lax.optimization_barrier((meta, out_grad[:, GRAD_FIRST:], first))[:2]
    first = swap_plane(first)
    meta = gather_z(meta)
    grads_all = gather_z(rest)
    first = mm(to_send, first, 1, 0).astype(bf16)
    meta, first = lax.optimization_barrier((meta, first))
    slots, slot_gate = lax.optimization_barrier(plane_slots(meta, plane))
    first = swap_z(lax.optimization_barrier((first, grads_all))[0])
    rows_in = mm(slots, tokens_all, 1, 0).astype(bf16)
    rows_in = swap_plane(rows_in)
    second = (mm(slots, grads_all, 1, 0) * slot_gate).astype(bf16)
    second = lax.optimization_barrier((second, first[1], first[2], rows_in))[0]
    second = swap_plane(second)
    first = weave(received, first)

    joined = mm(rows_in, w_in, 1, 0)
    d_hidden = mm(first, w_out[:, :GRAD_FIRST], 1, 1) + mm(second, w_out[:, GRAD_FIRST:], 1, 1)
    gate_part, up_part = joined[:, :half], joined[:, half:]
    activated, derivative = silu_parts(gate_part)
    hidden = (activated * up_part).astype(bf16)
    d_joined = jnp.concatenate([d_hidden * up_part * derivative, d_hidden * activated], axis=1).astype(bf16)

    back = swap_plane(mm(d_joined, w_in, 1, 1).astype(bf16))
    part = mm(slots, back, 0, 0).astype(bf16)
    token_grad = lax.psum_scatter(part, "z", scatter_dimension=0, tiled=True)

    grad_in = mm(rows_in, d_joined, 0, 0)
    grad_out = mm(hidden, jnp.concatenate([first, second], axis=1), 0, 0)
    half_width = width // 2
    other = 1 - core

    def sum_cores(x, axis):
        keep = lax.dynamic_slice_in_dim(x, core * half_width, half_width, axis)
        send = lax.dynamic_slice_in_dim(x, other * half_width, half_width, axis)
        got = lax.ppermute(send, "dp", [(0, 1), (1, 0)])
        return (keep + got).astype(bf16)[None]

    w_in_grad = sum_cores(grad_in, 0)
    w_out_grad = sum_cores(grad_out, 1)
    return token_grad, w_in_grad, w_out_grad


def solution(mesh):
    split = Mesh(mesh.devices.reshape(2, Z, X, Y), ("dp", "z", "x", "y"))
    hosts = ("z", "x", "y")
    rows = P(("dp",) + hosts, None)
    in_specs = (rows, rows, rows, rows, P(hosts, None, None), P(hosts, None, None))
    out_specs = (rows, P(hosts, "dp", None), P(hosts, None, "dp"))
    return jax.shard_map(body, mesh=split, in_specs=in_specs, out_specs=out_specs, check_vma=False)
```

```python
import jax
import jax.numpy as jnp
from jax import lax
from jax.experimental import pallas as pl
from jax.experimental.pallas import tpu as pltpu
from jax.sharding import Mesh
from jax.sharding import PartitionSpec as P

Z, X, Y = 8, 4, 4
PLANE = X * Y
CAP = 7
SLOTS = PLANE * CAP * Z
IN_FIRST = 384
GRAD_FIRST = 384

f32 = jnp.float32
bf16 = jnp.bfloat16


def mm(a, b, ca, cb):
    return lax.dot_general(a, b, (((ca,), (cb,)), ((), ())), preferred_element_type=f32)


def silu_parts(gate_part):
    sigma = 1.0 / (1.0 + jnp.exp(-gate_part))
    return gate_part * sigma, sigma * (1.0 + gate_part * (1.0 - sigma))


def rank_table(ids, gates, local):
    sources, _, tok = ids.shape
    match = ids[:, :, None, :] == local[None, None, :, None]
    named = jnp.any(match, axis=1)
    gate = jnp.sum(jnp.where(match, gates[:, :, None, :], 0.0), axis=1)
    index = jnp.arange(tok, dtype=jnp.int32)
    earlier = (index[:, None] < index[None, :]).astype(bf16)
    before = mm(named.astype(bf16).reshape(-1, tok), earlier, 1, 0)
    return jnp.where(named, before.reshape(named.shape), -1.0), gate


def plane_slots(meta, plane):
    tok = meta.shape[-1]
    meta = meta.reshape(Z, 8, tok)
    local = plane * PLANE + jnp.arange(PLANE, dtype=jnp.int32)
    rank, gate = rank_table(meta[:, :4].astype(jnp.int32), meta[:, 4:], local)
    rank, gate = rank.transpose(1, 0, 2), gate.transpose(1, 0, 2)
    slot_rank = jnp.arange(CAP, dtype=jnp.int32).astype(f32)
    hit = rank[:, None] == slot_rank[None, :, None, None]
    slot_gate = jnp.sum(jnp.where(hit, gate[:, None], 0.0), axis=3).reshape(-1, 1)
    same = jnp.arange(Z)[:, None] == jnp.arange(Z)[None, :]
    wide = jnp.where(same[None, :, :, None], rank[:, None], -1.0).reshape(PLANE, 1, Z, Z * tok)
    slots = (wide == slot_rank[None, :, None, None]).astype(bf16)
    return slots.reshape(SLOTS, Z * tok), slot_gate


def column_slots(ids, gates):
    tok = ids.shape[-1]
    rank, gate = rank_table(ids[None], gates[None], jnp.arange(Z * PLANE, dtype=jnp.int32))
    rank = rank.reshape(Z, PLANE, tok).transpose(1, 0, 2)
    gate = gate.reshape(Z, PLANE, tok).transpose(1, 0, 2)
    slot_rank = jnp.arange(CAP, dtype=jnp.int32).astype(f32)
    hit = rank[:, None] == slot_rank[None, :, None, None]
    slot_gate = jnp.sum(jnp.where(hit, gate[:, None], 0.0), axis=3).reshape(-1, 1)
    return hit.astype(bf16).reshape(SLOTS, tok), slot_gate


def order_matrices(plane):
    rows = PLANE * CAP
    by_distance = lax.broadcasted_iota(jnp.int32, (SLOTS, SLOTS), 0)
    by_plane = lax.broadcasted_iota(jnp.int32, (SLOTS, SLOTS), 1)
    same_row = by_plane // Z == by_distance % rows
    at = by_plane % Z
    distance = by_distance // rows
    to_send = same_row & (at == (plane + distance) % Z)
    by_plane, by_distance = by_distance, by_plane
    received = (by_plane // Z == by_distance % rows) & (by_plane % Z == (plane + Z - by_distance // rows) % Z)
    return to_send.astype(bf16), received.astype(bf16)


def times(name, matrix, parts, tile):
    width = parts[0].shape[1]

    def kernel(matrix_ref, *refs):
        stacked = jnp.concatenate([ref[...] for ref in refs[:-1]], axis=0)
        refs[-1][...] = jnp.dot(matrix_ref[...], stacked, preferred_element_type=f32).astype(bf16)

    return pl.pallas_call(
        kernel,
        grid=(width // tile,),
        in_specs=[pl.BlockSpec(matrix.shape, lambda i: (0, 0))] + [pl.BlockSpec((p.shape[0], tile), lambda i: (0, i)) for p in parts],
        out_specs=pl.BlockSpec((matrix.shape[0], tile), lambda i: (0, i)),
        out_shape=jax.ShapeDtypeStruct((matrix.shape[0], width), bf16),
        compiler_params=pltpu.CompilerParams(vmem_limit_bytes=24 * 2**20),
        name=name,
    )(matrix, *parts)


def weave(received, parts):
    return times("weave", received, parts, 384)


def body(tokens, out_grad, expert_ids, gate_weights, w_in, w_out):
    width = tokens.shape[1]
    w_in, w_out = w_in[0], w_out[0]
    half = w_out.shape[0]
    plane = lax.axis_index("z")
    core = lax.axis_index("dp")

    def gather_z(x):
        return lax.all_gather(x, "z", axis=0, tiled=True)

    def swap_plane(x):
        return lax.all_to_all(x, ("x", "y"), split_axis=0, concat_axis=0, tiled=True)

    def swap_z(x):
        rows = PLANE * CAP
        parts = [x[:rows]]
        for distance in range(1, Z):
            piece = x[distance * rows : (distance + 1) * rows]
            parts.append(lax.ppermute(piece, "z", [(i, (i + distance) % Z) for i in range(Z)]))
        return parts

    ids = expert_ids.T
    gates = gate_weights.T
    own_slots, own_gate = lax.optimization_barrier(column_slots(ids, gates))
    to_send, received = lax.optimization_barrier(order_matrices(plane))

    tokens_all = gather_z(tokens[:, IN_FIRST:])
    first_in = mm(own_slots, tokens[:, :IN_FIRST], 1, 0).astype(bf16)
    first_grad = (mm(own_slots, out_grad[:, :GRAD_FIRST], 1, 0) * own_gate).astype(bf16)
    first = jnp.concatenate([first_in, first_grad], axis=1)
    meta = jnp.concatenate([ids.astype(f32), gates], axis=0)
    meta, rest = lax.optimization_barrier((meta, out_grad[:, GRAD_FIRST:], first))[:2]
    first = swap_plane(first)
    meta = gather_z(meta)
    grads_all = gather_z(rest)
    first = mm(to_send, first, 1, 0).astype(bf16)
    meta, first = lax.optimization_barrier((meta, first))
    slots, slot_gate = lax.optimization_barrier(plane_slots(meta, plane))
    first = swap_z(lax.optimization_barrier((first, grads_all))[0])
    rows_in = swap_plane(mm(slots, tokens_all, 1, 0).astype(bf16))
    second = (mm(slots, grads_all, 1, 0) * slot_gate).astype(bf16)
    second = lax.optimization_barrier((second, first[1], first[2], rows_in))[0]
    second = swap_plane(second)
    joined = mm(rows_in, w_in[IN_FIRST:], 1, 0)
    first, joined = lax.optimization_barrier((first, joined))
    first = weave(received, first)
    first_in, first_grad = first[:, :IN_FIRST], first[:, IN_FIRST:]

    joined = joined + mm(first_in, w_in[:IN_FIRST], 1, 0)
    d_hidden = mm(first_grad, w_out[:, :GRAD_FIRST], 1, 1) + mm(second, w_out[:, GRAD_FIRST:], 1, 1)
    gate_part, up_part = joined[:, :half], joined[:, half:]
    activated, derivative = silu_parts(gate_part)
    hidden = (activated * up_part).astype(bf16)
    d_joined = jnp.concatenate([d_hidden * up_part * derivative, d_hidden * activated], axis=1).astype(bf16)

    back = swap_plane(mm(d_joined, w_in, 1, 1).astype(bf16))
    part = mm(slots, back, 0, 0).astype(bf16)
    token_grad = lax.psum_scatter(part, "z", scatter_dimension=0, tiled=True)

    grad_in = mm(jnp.concatenate([first_in, rows_in], axis=1), d_joined, 0, 0)
    grad_out = mm(hidden, jnp.concatenate([first_grad, second], axis=1), 0, 0)
    half_width = width // 2
    other = 1 - core

    def sum_cores(x, axis):
        keep = lax.dynamic_slice_in_dim(x, core * half_width, half_width, axis)
        send = lax.dynamic_slice_in_dim(x, other * half_width, half_width, axis)
        got = lax.ppermute(send, "dp", [(0, 1), (1, 0)])
        return (keep + got).astype(bf16)[None]

    w_in_grad = sum_cores(grad_in, 0)
    w_out_grad = sum_cores(grad_out, 1)
    return token_grad, w_in_grad, w_out_grad


def solution(mesh):
    split = Mesh(mesh.devices.reshape(2, Z, X, Y), ("dp", "z", "x", "y"))
    hosts = ("z", "x", "y")
    rows = P(("dp",) + hosts, None)
    in_specs = (rows, rows, rows, rows, P(hosts, None, None), P(hosts, None, None))
    out_specs = (rows, P(hosts, "dp", None), P(hosts, None, "dp"))
    return jax.shard_map(body, mesh=split, in_specs=in_specs, out_specs=out_specs, check_vma=False)
```
